32 devices in a mesh: mem: 4 (over y, x), ty: 4 (over z), tx: 2 (over core).
Axes of the slice: x: 2, y: 2, z: 4, core: 2. Of those that a mesh axis runs over, the one named last changes fastest.
Arguments:
- controls: float32 [16, 512, 1024], P(('mem', 'ty'), None, 'tx'), may hold values from -6 to 6
- perturbations: bfloat16 [16, 512, 1024], P(None, ('mem', 'ty'), 'tx'), may hold values from -6 to 6
- kx: bfloat16 [512, 1024], P(None, 'tx'), may hold values from 0.11 to 0.24
- ky: bfloat16 [512, 1024], P(None, 'tx'), may hold values from 0.11 to 0.24
- wet: int32 [512, 1024], P(None, 'tx'), may hold values from 0 to 1, as said below
Outputs:
- smoothed: float32 [16, 512, 1024], P(('mem', 'ty'), None, 'tx')
- increment: float32 [2, 512, 1024], P(None, ('mem', 'ty'), 'tx')
The draws below stay inside these ranges and needn't reach their ends.
Inputs may be any that keep to these rules, and one draw needn't show every extreme that they name: `wet`: rows 0 and 511 are land (0) in every column.
All inputs are finite; a program needn't handle non-finite values.
Results may differ from the reference program's by a relative error of at most 0.0003.
Values may be sent and summed in bfloat16 or wider, within the bound.
A program may use at most 64 MiB of HBM per device.

```python
import jax
import jax.numpy as jnp
from jax import lax

MEMBERS = 8
STEPS = 8
SLABS = 16
LEV = 2
NY = 512
NX = 1024


def draw_wet(key, part):
    cell_key, block_key = jax.random.split(key)
    cell_draw = jax.random.randint(cell_key, (NY, NX), 0, 100) < 98
    blocks = jax.random.randint(block_key, (NY // 4, NX // 4), 0, 100) < 99
    blocks = jnp.repeat(jnp.repeat(blocks, 4, axis=0), 4, axis=1)
    row_index = jnp.arange(NY)[:, None]
    interior = (row_index > 0) & (row_index < NY - 1)
    return (cell_draw & blocks & interior).astype(jnp.int32)


def coefficient_field(key, salt):
    uniform_draw = jax.random.uniform(jax.random.fold_in(key, salt), (NY, NX), jnp.float32)
    factor = 1.0 - 0.5 * uniform_draw * uniform_draw
    return (0.23925781 * factor).astype(jnp.bfloat16)


def draw_kx(key, part):
    return coefficient_field(key, 1101)


def draw_ky(key, part):
    return coefficient_field(key, 1202)


def draw_controls(key, part):
    noise_key = jax.random.fold_in(key, 1303)
    noise = jax.random.normal(noise_key, (SLABS, NY, NX), jnp.float32)
    row_index = jnp.arange(NY, dtype=jnp.int32)[:, None]
    col_index = jnp.arange(NX, dtype=jnp.int32)[None, :]
    parity = ((row_index + col_index) % 2).astype(jnp.float32)
    checker = 3.0 * (1.0 - 2.0 * parity)
    return jnp.clip(noise + checker[None, :, :], -6.0, 6.0)


def levels(rng, extent, shards, smallest, top_value):
    loudness, own = 1.0, jax.random.fold_in(rng, 6)
    for axis_at, blocks in shards:
        heights = jnp.exp(jax.random.uniform(jax.random.fold_in(own, axis_at), (blocks,), jnp.float32, smallest / len(shards), top_value / len(shards)))
        loudness = loudness * jnp.repeat(heights, extent[axis_at] // blocks).reshape([-1 if axis == axis_at else 1 for axis in range(len(extent))])
    return loudness


def normal_values(key, extent, deviation, limit, shards=(), kind=jnp.bfloat16):
    loudness = levels(key, extent, shards, -0.22, 0.18) if shards else 1.0
    array = jax.random.normal(key, extent, jnp.float32) * deviation * loudness
    return jnp.minimum(jnp.maximum(array, -limit), limit).astype(kind)


def setup_inputs(seed: int = 0) -> dict:
    key_of = jax.random.split(jax.random.key(seed), 6)
    controls = draw_controls(jax.random.fold_in(key_of[5], 71), 0)
    perturbations = normal_values(key_of[1], (SLABS, NY, NX), 1.0, 6.0, ((1, 16), (2, 2)))
    kx = draw_kx(jax.random.fold_in(key_of[5], 71), 0)
    ky = draw_ky(jax.random.fold_in(key_of[5], 71), 0)
    wet = draw_wet(jax.random.fold_in(key_of[5], 71), 0)
    return dict(controls=controls, perturbations=perturbations, kx=kx, ky=ky, wet=wet)


def reference(controls, perturbations, kx, ky, wet):
    ocean = wet.astype(jnp.float32)
    zonal_coef = kx.astype(jnp.float32) * ocean
    merid_coef = ky.astype(jnp.float32) * ocean
    face_east = jnp.minimum(zonal_coef, jnp.roll(zonal_coef, -1, 1))
    face_west = jnp.roll(face_east, 1, 1)
    zero_row = jnp.zeros((1, NX), jnp.float32)
    merid_next = jnp.concatenate([merid_coef[1:], zero_row], 0)
    face_north = jnp.minimum(merid_coef, merid_next)
    face_south = jnp.concatenate([zero_row, face_north[:-1]], 0)
    smoothed = controls
    zero_slab = jnp.zeros((SLABS, 1, NX), jnp.float32)
    for step_index in range(STEPS):
        east_cell = jnp.roll(smoothed, -1, 2)
        west_cell = jnp.roll(smoothed, 1, 2)
        north_cell = jnp.concatenate([smoothed[:, 1:], zero_slab], 1)
        south_cell = jnp.concatenate([zero_slab, smoothed[:, :-1]], 1)
        smoothed = smoothed + (face_east * (east_cell - smoothed) - face_west * (smoothed - west_cell)) + (face_north * (north_cell - smoothed) - face_south * (smoothed - south_cell))
    member_scale = 1.0 / jnp.sqrt(jnp.float32(MEMBERS - 1))
    product = perturbations.astype(jnp.float32).reshape(MEMBERS, LEV, NY, NX) * smoothed.reshape(MEMBERS, LEV, NY, NX)
    increment = lax.optimization_barrier(jnp.sum(product, axis=0)) * member_scale
    return (smoothed, increment)
```

```python
import functools
import math

import jax
import jax.numpy as jnp
from jax import lax
from jax.experimental import pallas as pl
from jax.experimental.pallas import tpu as pltpu
from jax.sharding import PartitionSpec as P

MEMBERS = 8
STEPS = 8
LANES = 128
GROUP = 8
WIRE = jnp.float32
WIRE_SCALE = 1.0
MESH = pl.DeviceIdType.MESH


def kernel(
    mems, tys, txs, ctrl, pert, kx, ky, wet, out_s, out_i,
    f_in, kx_in, ky_in, wet_in, pert_in, edge_f, edge_g, halo_f, halo_g,
    gx_all, gy_all, fields, fe, fn, send, recv,
    in_sem, out_sem, edge_send, edge_recv, tile_send, tile_recv,
):
    tiles = mems * tys
    rows, cols = f_in.shape
    wide = cols + LANES
    tile = rows // tiles
    levels = tiles // MEMBERS
    lead = GROUP * (STEPS + 1)
    warm = GROUP * STEPS // tile
    me_mem, me_ty, me_tx = lax.axis_index("mem"), lax.axis_index("ty"), lax.axis_index("tx")
    me = me_mem * tys + me_ty
    first = me + 1
    right, left = lax.rem(me_tx + 1, txs), lax.rem(me_tx + txs - 1, txs)
    sides = (right,) if txs == 2 else (right, left)

    loads = [
        pltpu.make_async_copy(src, dst, in_sem.at[n])
        for n, (src, dst) in enumerate(
            ((kx, kx_in), (ky, ky_in), (wet, wet_in), (ctrl.at[0], f_in), (pert, pert_in))
        )
    ]
    for load in loads:
        load.start()

    barrier = pltpu.get_barrier_semaphore()
    for side in sides:
        pl.semaphore_signal(barrier, inc=1, device_id={"tx": side}, device_id_type=MESH)

    @pl.loop(1, tiles)
    def _(step):
        to = lax.rem(me + step, tiles)
        pl.semaphore_signal(
            barrier, inc=1, device_id={"mem": to // tys, "ty": lax.rem(to, tys)}, device_id_type=MESH
        )

    lane = lax.broadcasted_iota(jnp.int32, (1, LANES), 1)
    low = lane < LANES // 2
    for load in loads[:3]:
        load.wait()
    chunk = 32

    @pl.loop(0, rows // chunk)
    def _(n):
        at = pl.ds(pl.multiple_of(n * chunk, chunk), chunk)
        ocean = wet_in[at, :].astype(jnp.float32)
        gx = kx_in[at, :].astype(jnp.float32) * ocean
        gy = ky_in[at, :].astype(jnp.float32) * ocean
        gx_all[at, :cols] = gx
        gy_all[at, :cols] = gy
        edge_g[0, at, :] = jnp.where(low, gx[:, :LANES], gx[:, cols - LANES :]).astype(jnp.bfloat16)
        edge_g[1, at, :] = jnp.where(low, gy[:, :LANES], gy[:, cols - LANES :]).astype(jnp.bfloat16)

    gy_all[rows:, :] = jnp.zeros((GROUP, wide), jnp.float32)
    loads[3].wait()

    @pl.loop(0, rows // chunk)
    def _(n):
        at = pl.ds(pl.multiple_of(n * chunk, chunk), chunk)
        edge_f[at, :] = jnp.where(low, f_in[at, :LANES], f_in[at, cols - LANES :])

    pl.semaphore_wait(barrier, tiles - 1 + len(sides))
    edges = []
    for n, side in enumerate(sides):
        for m, (src, dst) in enumerate(((edge_g, halo_g), (edge_f, halo_f))):
            edges.append(
                pltpu.make_async_remote_copy(
                    src_ref=src, dst_ref=dst.at[n],
                    send_sem=edge_send.at[n, m], recv_sem=edge_recv.at[n, m],
                    device_id={"tx": side}, device_id_type=MESH,
                )
            )
            edges[-1].start()

    @pl.loop(0, tiles + 2)
    def _(n):
        at = pl.multiple_of(lax.rem(first - 1 + n + tiles, tiles) * tile, tile)
        to = pl.multiple_of(lead + (n - 1) * tile, GROUP)
        fields[0, pl.ds(to, tile), :cols] = f_in[pl.ds(at, tile), :]

    for edge in edges:
        edge.wait_recv()

    east, west = len(sides) - 1, 0

    @pl.loop(0, rows // chunk)
    def _(n):
        at = pl.ds(pl.multiple_of(n * chunk, chunk), chunk)
        for c, whole in ((0, gx_all), (1, gy_all)):
            whole[at, cols:] = jnp.where(
                low, halo_g[east, c, at, :].astype(jnp.float32), halo_g[west, c, at, :].astype(jnp.float32)
            )

    @pl.loop(0, tiles + 2)
    def _(n):
        at = pl.multiple_of(lax.rem(first - 1 + n + tiles, tiles) * tile, tile)
        to = pl.ds(pl.multiple_of(lead + (n - 1) * tile, GROUP), tile)
        fields[0, to, cols:] = jnp.where(low, halo_f[east, pl.ds(at, tile), :], halo_f[west, pl.ds(at, tile), :])
        gx = gx_all[pl.ds(at, tile), :]
        fe[to, :] = jnp.minimum(gx, pltpu.roll(gx, wide - 1, 1))
        gy = gy_all[pl.ds(at, tile + GROUP), :]
        fn[to, :] = jnp.minimum(gy, pltpu.roll(gy, tile + GROUP - 1, 0))[:tile]

    sub = lax.broadcasted_iota(jnp.int32, (GROUP, wide), 0)
    top, bottom = sub == GROUP - 1, sub == 0

    def advance(k, base):
        src, dst = fields.at[k - 1], fields.at[k]

        def at(g):
            return pl.ds(pl.multiple_of(base + g * GROUP, GROUP), GROUP)

        prev = src[at(-1), :]
        cur = src[at(0), :]
        up = pltpu.roll(cur, GROUP - 1, 0)
        north = jnp.where(top, up, pltpu.roll(prev, GROUP - 1, 0))
        flux_before = pltpu.roll(fn[at(-1), :] * (north - prev), 1, 0)
        for g in range(tile // GROUP):
            following = src[at(g + 1), :]
            up_next = pltpu.roll(following, GROUP - 1, 0)
            north = jnp.where(top, up_next, up)
            flux_n = fn[at(g), :] * (north - cur)
            turned = pltpu.roll(flux_n, 1, 0)
            flux_s = jnp.where(bottom, flux_before, turned)
            flux_e = fe[at(g), :] * (pltpu.roll(cur, wide - 1, 1) - cur)
            flux_w = pltpu.roll(flux_e, 1, 1)
            dst[at(g), :] = cur + (flux_e - flux_w) + (flux_n - flux_s)
            cur, up, flux_before = following, up_next, turned

    def out_copy(t):
        to = lax.rem(first + t, tiles)
        return pltpu.make_async_copy(
            fields.at[STEPS, pl.ds(pl.multiple_of(lead + t * tile, GROUP), tile), pl.ds(0, cols)],
            out_s.at[0, pl.ds(pl.multiple_of(to * tile, tile), tile), :],
            out_sem.at[t],
        )

    def tile_copy(t):
        to = lax.rem(first + t, tiles)
        return pltpu.make_async_remote_copy(
            src_ref=send.at[t], dst_ref=recv.at[t],
            send_sem=tile_send.at[t], recv_sem=tile_recv.at[t],
            device_id={"mem": to // tys, "ty": lax.rem(to, tys)}, device_id_type=MESH,
        )

    @pl.loop(0, tiles + warm)
    def _(i):
        for k in range(1, STEPS + 1):
            advance(k, lead + i * tile - GROUP * k)

        @pl.when(i >= warm)
        def _():
            t = i - warm
            out_copy(t).start()

            @pl.when(t < tiles - 1)
            def _():
                done = fields[STEPS, pl.ds(pl.multiple_of(lead + t * tile, GROUP), tile), :cols]
                send[t] = (done * WIRE_SCALE).astype(WIRE)
                tile_copy(t).start()

    loads[4].wait()
    scale = 1.0 / math.sqrt(MEMBERS - 1)
    for level in range(levels):
        out_i[level] = jnp.zeros((tile, cols), jnp.float32)
    mine = fields[STEPS, lead + (tiles - 1) * tile : lead + tiles * tile, :cols]
    out_i[lax.rem(me, levels)] = pert_in[me].astype(jnp.float32) * (mine * scale)

    @pl.loop(0, tiles - 1)
    def _(t):
        tile_copy(t).wait_recv()
        slab = lax.rem(me - 1 - t + 2 * tiles, tiles)
        got = recv[t].astype(jnp.float32) * (scale / WIRE_SCALE)
        level = lax.rem(slab, levels)
        out_i[level] = out_i[level] + pert_in[slab].astype(jnp.float32) * got

    for edge in edges:
        edge.wait_send()

    @pl.loop(0, tiles)
    def _(t):
        out_copy(t).wait()

    @pl.loop(0, tiles - 1)
    def _(t):
        tile_copy(t).wait_send()


def solution(mesh):
    mems, tys, txs = mesh.shape["mem"], mesh.shape["ty"], mesh.shape["tx"]
    tiles = mems * tys

    def on_device(controls, perturbations, kx, ky, wet):
        rows, cols = kx.shape
        tile = rows // tiles
        levels = tiles // MEMBERS
        wide = cols + LANES
        lead = GROUP * (STEPS + 1)
        deep = lead + rows + GROUP * STEPS
        sides = 1 if txs == 2 else 2
        f32, bf16 = jnp.float32, jnp.bfloat16
        DMA = pltpu.SemaphoreType.DMA
        return pl.pallas_call(
            functools.partial(kernel, mems, tys, txs),
            out_shape=(
                jax.ShapeDtypeStruct((1, rows, cols), f32),
                jax.ShapeDtypeStruct((levels, tile, cols), f32),
            ),
            in_specs=[pl.BlockSpec(memory_space=pltpu.HBM)] * 5,
            out_specs=(pl.BlockSpec(memory_space=pl.ANY), pl.BlockSpec(memory_space=pltpu.VMEM)),
            scratch_shapes=[
                pltpu.VMEM((rows, cols), f32),
                pltpu.VMEM((rows, cols), bf16),
                pltpu.VMEM((rows, cols), bf16),
                pltpu.VMEM((rows, cols), jnp.int32),
                pltpu.VMEM((tiles, tile, cols), bf16),
                pltpu.VMEM((rows, LANES), f32),
                pltpu.VMEM((2, rows, LANES), bf16),
                pltpu.VMEM((sides, rows, LANES), f32),
                pltpu.VMEM((sides, 2, rows, LANES), bf16),
                pltpu.VMEM((rows, wide), f32),
                pltpu.VMEM((rows + GROUP, wide), f32),
                pltpu.VMEM((STEPS + 1, deep, wide), f32),
                pltpu.VMEM((deep, wide), f32),
                pltpu.VMEM((deep, wide), f32),
                pltpu.VMEM((tiles, tile, cols), WIRE),
                pltpu.VMEM((tiles, tile, cols), WIRE),
                DMA((5,)),
                DMA((tiles,)),
                DMA((sides, 2)),
                DMA((sides, 2)),
                DMA((tiles,)),
                DMA((tiles,)),
            ],
            compiler_params=pltpu.CompilerParams(
                collective_id=0, has_side_effects=True, vmem_limit_bytes=48 * 2**20
            ),
        )(controls, perturbations, kx, ky, wet)

    in_specs = (
        P(("mem", "ty"), None, "tx"),
        P(None, ("mem", "ty"), "tx"),
        P(None, "tx"),
        P(None, "tx"),
        P(None, "tx"),
    )
    out_specs = (P(("mem", "ty"), None, "tx"), P(None, ("mem", "ty"), "tx"))
    return jax.shard_map(
        on_device, mesh=mesh, in_specs=in_specs, out_specs=out_specs, check_vma=False
    )
```

```python
import functools
import math

import jax
import jax.numpy as jnp
from jax import lax
from jax.experimental import pallas as pl
from jax.experimental.pallas import tpu as pltpu
from jax.sharding import PartitionSpec as P

MEMBERS = 8
STEPS = 8
LANES = 128
GROUP = 8
BLOCK = 1
CODE = 32767.0
MESH = pl.DeviceIdType.MESH


def kernel(
    mems, tys, txs, ctrl, pert, kx, ky, wet, out_s, out_i,
    f_in, kx_in, ky_in, wet_in, pert_in, edge_f, edge_g, halo_f, halo_g,
    gx_all, gy_all, fe, fn, send, recv, peak, peaks,
    in_sem, out_sem, edge_send, edge_recv, tile_send, tile_recv, peak_send, peak_recv,
    start, final, *carries,
):
    tiles = mems * tys
    rows, cols = f_in.shape
    wide = cols + LANES
    tile = rows // tiles
    levels = tiles // MEMBERS
    lead = GROUP * (STEPS + 1)
    warm = GROUP * STEPS // (BLOCK * tile)
    me_mem, me_ty, me_tx = lax.axis_index("mem"), lax.axis_index("ty"), lax.axis_index("tx")
    me = me_mem * tys + me_ty
    first = me + 1
    right, left = lax.rem(me_tx + 1, txs), lax.rem(me_tx + txs - 1, txs)
    sides = (right,) if txs == 2 else (right, left)

    loads = [
        pltpu.make_async_copy(src, dst, in_sem.at[n])
        for n, (src, dst) in enumerate(
            ((kx, kx_in), (ky, ky_in), (wet, wet_in), (ctrl.at[0], f_in), (pert, pert_in))
        )
    ]
    for load in loads:
        load.start()

    barrier = pltpu.get_barrier_semaphore()
    for side in sides:
        pl.semaphore_signal(barrier, inc=1, device_id={"tx": side}, device_id_type=MESH)

    @pl.loop(1, tiles)
    def _(step):
        to = lax.rem(me + step, tiles)
        pl.semaphore_signal(
            barrier, inc=1, device_id={"mem": to // tys, "ty": lax.rem(to, tys)}, device_id_type=MESH
        )

    lane = lax.broadcasted_iota(jnp.int32, (1, LANES), 1)
    low = lane < LANES // 2
    for load in loads[:3]:
        load.wait()
    chunk = 32

    @pl.loop(0, rows // chunk)
    def _(n):
        at = pl.ds(pl.multiple_of(n * chunk, chunk), chunk)
        ocean = wet_in[at, :].astype(jnp.float32)
        gx = kx_in[at, :].astype(jnp.float32) * ocean
        gy = ky_in[at, :].astype(jnp.float32) * ocean
        gx_all[at, :cols] = gx
        gy_all[at, :cols] = gy
        edge_g[0, at, :] = jnp.where(low, gx[:, :LANES], gx[:, cols - LANES :]).astype(jnp.bfloat16)
        edge_g[1, at, :] = jnp.where(low, gy[:, :LANES], gy[:, cols - LANES :]).astype(jnp.bfloat16)

    gy_all[rows:, :] = jnp.zeros((GROUP, wide), jnp.float32)
    loads[3].wait()

    @pl.loop(0, rows // chunk)
    def _(n):
        at = pl.ds(pl.multiple_of(n * chunk, chunk), chunk)
        edge_f[at, :] = jnp.where(low, f_in[at, :LANES], f_in[at, cols - LANES :])

    pl.semaphore_wait(barrier, tiles - 1 + len(sides))
    edges = []
    for n, side in enumerate(sides):
        for m, (src, dst) in enumerate(((edge_g, halo_g), (edge_f, halo_f))):
            edges.append(
                pltpu.make_async_remote_copy(
                    src_ref=src, dst_ref=dst.at[n],
                    send_sem=edge_send.at[n, m], recv_sem=edge_recv.at[n, m],
                    device_id={"tx": side}, device_id_type=MESH,
                )
            )
            edges[-1].start()

    @pl.loop(0, tiles + 2)
    def _(n):
        at = pl.multiple_of(lax.rem(first - 1 + n + tiles, tiles) * tile, tile)
        to = pl.multiple_of(lead + (n - 1) * tile, GROUP)
        start[pl.ds(to, tile), :cols] = f_in[pl.ds(at, tile), :]

    for edge in edges:
        edge.wait_recv()

    east, west = len(sides) - 1, 0

    @pl.loop(0, rows // chunk)
    def _(n):
        at = pl.ds(pl.multiple_of(n * chunk, chunk), chunk)
        for c, whole in ((0, gx_all), (1, gy_all)):
            whole[at, cols:] = jnp.where(
                low, halo_g[east, c, at, :].astype(jnp.float32), halo_g[west, c, at, :].astype(jnp.float32)
            )

    @pl.loop(0, tiles + 2)
    def _(n):
        at = pl.multiple_of(lax.rem(first - 1 + n + tiles, tiles) * tile, tile)
        to = pl.ds(pl.multiple_of(lead + (n - 1) * tile, GROUP), tile)
        start[to, cols:] = jnp.where(low, halo_f[east, pl.ds(at, tile), :], halo_f[west, pl.ds(at, tile), :])
        gx = gx_all[pl.ds(at, tile), :]
        fe[to, :] = jnp.minimum(gx, pltpu.roll(gx, wide - 1, 1))
        gy = gy_all[pl.ds(at, tile + GROUP), :]
        fn[to, :] = jnp.minimum(gy, pltpu.roll(gy, tile + GROUP - 1, 0))[:tile]

    def largest(n, most):
        at = pl.ds(pl.multiple_of(lead + n * tile, GROUP), tile)
        return jnp.maximum(most, jnp.abs(start[at, :]))

    most = lax.fori_loop(0, tiles, largest, jnp.full((tile, wide), 1e-30, jnp.float32))
    most = jnp.max(jnp.max(most, axis=0, keepdims=True), axis=1, keepdims=True)
    peak[...] = jnp.broadcast_to(most, (GROUP, LANES))

    def peak_copy(t):
        to = lax.rem(first + t, tiles)
        return pltpu.make_async_remote_copy(
            src_ref=peak, dst_ref=peaks.at[t],
            send_sem=peak_send.at[t], recv_sem=peak_recv.at[t],
            device_id={"mem": to // tys, "ty": lax.rem(to, tys)}, device_id_type=MESH,
        )

    @pl.loop(0, tiles - 1)
    def _(t):
        peak_copy(t).start()

    sub = lax.broadcasted_iota(jnp.int32, (GROUP, wide), 0)
    top, bottom = sub == GROUP - 1, sub == 0

    block = BLOCK * tile
    groups = block // GROUP

    def advance(k, base, fresh):
        def at(g):
            return pl.ds(pl.multiple_of(base + g * GROUP, GROUP), GROUP)

        if k == 1:
            cells = [start[at(g), :] for g in range(-1, groups + 1)]
        else:
            kept = carries[k - 2]
            cells = [kept[:GROUP, :], kept[GROUP:, :]] + fresh
        fluxes = [None] * (groups + 1)
        turned = [None] * (groups + 1)
        ups = [pltpu.roll(cell, GROUP - 1, 0) for cell in cells]
        for g in range(groups + 1):
            north = jnp.where(top, ups[g + 1], ups[g])
            fluxes[g] = fn[at(g - 1), :] * (north - cells[g])
            turned[g] = pltpu.roll(fluxes[g], 1, 0)
        results = []
        for g in range(1, groups + 1):
            cur = cells[g]
            flux_s = jnp.where(bottom, turned[g - 1], turned[g])
            flux_e = fe[at(g - 1), :] * (pltpu.roll(cur, wide - 1, 1) - cur)
            flux_w = pltpu.roll(flux_e, 1, 1)
            results.append(cur + (flux_e - flux_w) + (fluxes[g] - flux_s))
        if k < STEPS:
            kept = carries[k - 1]
            return results, (kept, results[groups - 2], results[groups - 1])
        for g in range(groups):
            final[at(g), :] = results[g]
        return results, None

    def out_copy(t):
        to = lax.rem(first + t, tiles)
        return pltpu.make_async_copy(
            final.at[pl.ds(pl.multiple_of(lead + t * tile, GROUP), tile), pl.ds(0, cols)],
            out_s.at[0, pl.ds(pl.multiple_of(to * tile, tile), tile), :],
            out_sem.at[t],
        )

    def tile_copy(t):
        to = lax.rem(first + t, tiles)
        return pltpu.make_async_remote_copy(
            src_ref=send.at[t], dst_ref=recv.at[t],
            send_sem=tile_send.at[t], recv_sem=tile_recv.at[t],
            device_id={"mem": to // tys, "ty": lax.rem(to, tys)}, device_id_type=MESH,
        )

    def finish(t):
        out_copy(t).start()

        @pl.when(t < tiles - 1)
        def _():
            done = final[pl.ds(pl.multiple_of(lead + t * tile, GROUP), tile), :cols]
            size = jnp.sqrt(jnp.abs(done) * (CODE * CODE / peak[:1, :1]))
            size = jnp.minimum(size + 0.5, CODE).astype(jnp.int32)
            send[t] = jnp.where(done < 0, -size, size).astype(jnp.int16)
            tile_copy(t).start()

    @pl.loop(0, tiles // BLOCK + warm)
    def _(i):
        fresh, saves = None, []
        for k in range(1, STEPS + 1):
            fresh, save = advance(k, lead + i * block - GROUP * k, fresh)
            saves.append(save)
        for kept, before, last in saves[:-1]:
            kept[:GROUP, :] = before
            kept[GROUP:, :] = last

        @pl.when(i >= warm)
        def _():
            for n in range(BLOCK):
                finish((i - warm) * BLOCK + n)

    loads[4].wait()
    scale = 1.0 / math.sqrt(MEMBERS - 1)
    for level in range(levels):
        out_i[level] = jnp.zeros((tile, cols), jnp.float32)
    mine = final[lead + (tiles - 1) * tile : lead + tiles * tile, :cols]
    out_i[lax.rem(me, levels)] = pert_in[me].astype(jnp.float32) * (mine * scale)

    @pl.loop(0, tiles - 1)
    def _(t):
        tile_copy(t).wait_recv()
        slab = lax.rem(me - 1 - t + 2 * tiles, tiles)
        peak_copy(t).wait_recv()
        code = recv[t].astype(jnp.float32)
        got = code * jnp.abs(code) * (peaks[t, :1, :1] * (scale / (CODE * CODE)))
        level = lax.rem(slab, levels)
        out_i[level] = out_i[level] + pert_in[slab].astype(jnp.float32) * got

    for edge in edges:
        edge.wait_send()

    @pl.loop(0, tiles)
    def _(t):
        out_copy(t).wait()

    @pl.loop(0, tiles - 1)
    def _(t):
        tile_copy(t).wait_send()
        peak_copy(t).wait_send()


def solution(mesh):
    mems, tys, txs = mesh.shape["mem"], mesh.shape["ty"], mesh.shape["tx"]
    tiles = mems * tys

    def on_device(controls, perturbations, kx, ky, wet):
        rows, cols = kx.shape
        tile = rows // tiles
        levels = tiles // MEMBERS
        wide = cols + LANES
        lead = GROUP * (STEPS + 1)
        deep = lead + rows + GROUP * STEPS
        sides = 1 if txs == 2 else 2
        f32, bf16 = jnp.float32, jnp.bfloat16
        DMA = pltpu.SemaphoreType.DMA
        return pl.pallas_call(
            functools.partial(kernel, mems, tys, txs),
            out_shape=(
                jax.ShapeDtypeStruct((1, rows, cols), f32),
                jax.ShapeDtypeStruct((levels, tile, cols), f32),
            ),
            in_specs=[pl.BlockSpec(memory_space=pltpu.HBM)] * 5,
            out_specs=(pl.BlockSpec(memory_space=pl.ANY), pl.BlockSpec(memory_space=pltpu.VMEM)),
            scratch_shapes=[
                pltpu.VMEM((rows, cols), f32),
                pltpu.VMEM((rows, cols), bf16),
                pltpu.VMEM((rows, cols), bf16),
                pltpu.VMEM((rows, cols), jnp.int32),
                pltpu.VMEM((tiles, tile, cols), bf16),
                pltpu.VMEM((rows, LANES), f32),
                pltpu.VMEM((2, rows, LANES), bf16),
                pltpu.VMEM((sides, rows, LANES), f32),
                pltpu.VMEM((sides, 2, rows, LANES), bf16),
                pltpu.VMEM((rows, wide), f32),
                pltpu.VMEM((rows + GROUP, wide), f32),
                pltpu.VMEM((deep, wide), f32),
                pltpu.VMEM((deep, wide), f32),
                pltpu.VMEM((tiles, tile, cols), jnp.int16),
                pltpu.VMEM((tiles, tile, cols), jnp.int16),
                pltpu.VMEM((GROUP, LANES), f32),
                pltpu.VMEM((tiles, GROUP, LANES), f32),
                DMA((5,)),
                DMA((tiles,)),
                DMA((sides, 2)),
                DMA((sides, 2)),
                DMA((tiles,)),
                DMA((tiles,)),
                DMA((tiles,)),
                DMA((tiles,)),
                pltpu.VMEM((deep, wide), f32),
                pltpu.VMEM((deep, wide), f32),
                *[pltpu.VMEM((2 * GROUP, wide), f32)] * (STEPS - 1),
            ],
            compiler_params=pltpu.CompilerParams(
                collective_id=0, has_side_effects=True, vmem_limit_bytes=63 * 2**20
            ),
        )(controls, perturbations, kx, ky, wet)

    in_specs = (
        P(("mem", "ty"), None, "tx"),
        P(None, ("mem", "ty"), "tx"),
        P(None, "tx"),
        P(None, "tx"),
        P(None, "tx"),
    )
    out_specs = (P(("mem", "ty"), None, "tx"), P(None, ("mem", "ty"), "tx"))
    return jax.shard_map(
        on_device, mesh=mesh, in_specs=in_specs, out_specs=out_specs, check_vma=False
    )
```

```python
import functools
import math

import jax
import jax.numpy as jnp
from jax import lax
from jax.experimental import pallas as pl
from jax.experimental.pallas import tpu as pltpu
from jax.sharding import PartitionSpec as P

MEMBERS = 8
STEPS = 8
LANES = 128
GROUP = 8
BLOCK = 1
CODE = 32767.0
MESH = pl.DeviceIdType.MESH


def kernel(
    mems, tys, txs, ctrl, pert, kx, ky, wet, out_s, out_i,
    f_in, kx_in, ky_in, wet_in, pert_in, edge_f, edge_g, halo_f, halo_g,
    gx_all, gy_all, fe, fn, send, recv, peak, peaks,
    in_sem, out_sem, edge_send, edge_recv, tile_send, tile_recv, peak_send, peak_recv,
    start, final, *carries,
):
    tiles = mems * tys
    rows, cols = f_in.shape
    wide = cols + LANES
    tile = rows // tiles
    levels = tiles // MEMBERS
    lead = GROUP * (STEPS + 1)
    warm = GROUP * STEPS // (BLOCK * tile)
    me_mem, me_ty, me_tx = lax.axis_index("mem"), lax.axis_index("ty"), lax.axis_index("tx")
    me = me_mem * tys + me_ty
    first = me + 1
    right, left = lax.rem(me_tx + 1, txs), lax.rem(me_tx + txs - 1, txs)
    sides = (right,) if txs == 2 else (right, left)

    loads = [
        pltpu.make_async_copy(src, dst, in_sem.at[n])
        for n, (src, dst) in enumerate(
            ((kx, kx_in), (ky, ky_in), (wet, wet_in), (ctrl.at[0], f_in), (pert, pert_in))
        )
    ]
    for load in loads:
        load.start()

    barrier = pltpu.get_barrier_semaphore()
    for side in sides:
        pl.semaphore_signal(barrier, inc=1, device_id={"tx": side}, device_id_type=MESH)

    @pl.loop(1, tiles)
    def _(step):
        to = lax.rem(me + step, tiles)
        pl.semaphore_signal(
            barrier, inc=1, device_id={"mem": to // tys, "ty": lax.rem(to, tys)}, device_id_type=MESH
        )

    lane = lax.broadcasted_iota(jnp.int32, (1, LANES), 1)
    low = lane < LANES // 2
    for load in loads[:3]:
        load.wait()
    chunk = 32

    @pl.loop(0, rows // chunk)
    def _(n):
        at = pl.ds(pl.multiple_of(n * chunk, chunk), chunk)
        ocean = wet_in[at, :].astype(jnp.float32)
        gx = kx_in[at, :].astype(jnp.float32) * ocean
        gy = ky_in[at, :].astype(jnp.float32) * ocean
        gx_all[at, :cols] = gx
        gy_all[at, :cols] = gy
        edge_g[0, at, :] = jnp.where(low, gx[:, :LANES], gx[:, cols - LANES :]).astype(jnp.bfloat16)
        edge_g[1, at, :] = jnp.where(low, gy[:, :LANES], gy[:, cols - LANES :]).astype(jnp.bfloat16)

    gy_all[rows:, :] = jnp.zeros((GROUP, wide), jnp.float32)
    loads[3].wait()

    @pl.loop(0, rows // chunk)
    def _(n):
        at = pl.ds(pl.multiple_of(n * chunk, chunk), chunk)
        edge_f[at, :] = jnp.where(low, f_in[at, :LANES], f_in[at, cols - LANES :])

    pl.semaphore_wait(barrier, tiles - 1 + len(sides))
    edges = []
    for n, side in enumerate(sides):
        for m, (src, dst) in enumerate(((edge_g, halo_g), (edge_f, halo_f))):
            edges.append(
                pltpu.make_async_remote_copy(
                    src_ref=src, dst_ref=dst.at[n],
                    send_sem=edge_send.at[n, m], recv_sem=edge_recv.at[n, m],
                    device_id={"tx": side}, device_id_type=MESH,
                )
            )
            edges[-1].start()

    @pl.loop(0, tiles + 2)
    def _(n):
        at = pl.multiple_of(lax.rem(first - 1 + n + tiles, tiles) * tile, tile)
        to = pl.multiple_of(lead + (n - 1) * tile, GROUP)
        start[pl.ds(to, tile), :cols] = f_in[pl.ds(at, tile), :]

    for edge in edges:
        edge.wait_recv()

    east, west = len(sides) - 1, 0

    @pl.loop(0, rows // chunk)
    def _(n):
        at = pl.ds(pl.multiple_of(n * chunk, chunk), chunk)
        for c, whole in ((0, gx_all), (1, gy_all)):
            whole[at, cols:] = jnp.where(
                low, halo_g[east, c, at, :].astype(jnp.float32), halo_g[west, c, at, :].astype(jnp.float32)
            )

    @pl.loop(0, tiles + 2)
    def _(n):
        at = pl.multiple_of(lax.rem(first - 1 + n + tiles, tiles) * tile, tile)
        to = pl.ds(pl.multiple_of(lead + (n - 1) * tile, GROUP), tile)
        start[to, cols:] = jnp.where(low, halo_f[east, pl.ds(at, tile), :], halo_f[west, pl.ds(at, tile), :])
        gx = gx_all[pl.ds(at, tile), :]
        fe[to, :] = jnp.minimum(gx, pltpu.roll(gx, wide - 1, 1))
        gy = gy_all[pl.ds(at, tile + GROUP), :]
        fn[to, :] = jnp.minimum(gy, pltpu.roll(gy, tile + GROUP - 1, 0))[:tile]

    def largest(n, most):
        at = pl.ds(pl.multiple_of(lead + n * tile, GROUP), tile)
        return jnp.maximum(most, jnp.abs(start[at, :]))

    most = lax.fori_loop(0, tiles, largest, jnp.full((tile, wide), 1e-30, jnp.float32))
    most = jnp.max(jnp.max(most, axis=0, keepdims=True), axis=1, keepdims=True)
    peak[...] = jnp.broadcast_to(most, (GROUP, LANES))

    def peak_copy(t):
        to = lax.rem(first + t, tiles)
        return pltpu.make_async_remote_copy(
            src_ref=peak, dst_ref=peaks.at[t],
            send_sem=peak_send.at[t], recv_sem=peak_recv.at[t],
            device_id={"mem": to // tys, "ty": lax.rem(to, tys)}, device_id_type=MESH,
        )

    @pl.loop(0, tiles - 1)
    def _(t):
        peak_copy(t).start()

    sub = lax.broadcasted_iota(jnp.int32, (GROUP, wide), 0)
    top, bottom = sub == GROUP - 1, sub == 0

    block = BLOCK * tile
    groups = block // GROUP

    def advance(k, base, fresh):
        def at(g):
            return pl.ds(pl.multiple_of(base + g * GROUP, GROUP), GROUP)

        if k == 1:
            cells = [start[at(g), :] for g in range(-1, groups + 1)]
        else:
            kept = carries[k - 2]
            cells = [kept[:GROUP, :], kept[GROUP:, :]] + fresh
        fluxes = [None] * (groups + 1)
        turned = [None] * (groups + 1)
        ups = [pltpu.roll(cell, GROUP - 1, 0) for cell in cells]
        for g in range(groups + 1):
            north = jnp.where(top, ups[g + 1], ups[g])
            fluxes[g] = fn[at(g - 1), :] * (north - cells[g])
            turned[g] = pltpu.roll(fluxes[g], 1, 0)
        results = []
        for g in range(1, groups + 1):
            cur = cells[g]
            flux_s = jnp.where(bottom, turned[g - 1], turned[g])
            flux_e = fe[at(g - 1), :] * (pltpu.roll(cur, wide - 1, 1) - cur)
            flux_w = pltpu.roll(flux_e, 1, 1)
            results.append(cur + (flux_e - flux_w) + (fluxes[g] - flux_s))
        if k < STEPS:
            kept = carries[k - 1]
            return results, (kept, results[groups - 2], results[groups - 1])
        for g in range(groups):
            final[at(g), :] = results[g]
        return results, None

    def out_copy(t):
        to = lax.rem(first + t, tiles)
        return pltpu.make_async_copy(
            final.at[pl.ds(pl.multiple_of(lead + t * tile, GROUP), tile), pl.ds(0, cols)],
            out_s.at[0, pl.ds(pl.multiple_of(to * tile, tile), tile), :],
            out_sem.at[t],
        )

    def tile_copy(t):
        to = lax.rem(first + t, tiles)
        return pltpu.make_async_remote_copy(
            src_ref=send.at[t], dst_ref=recv.at[t],
            send_sem=tile_send.at[t], recv_sem=tile_recv.at[t],
            device_id={"mem": to // tys, "ty": lax.rem(to, tys)}, device_id_type=MESH,
        )

    def finish(t):
        out_copy(t).start()

        @pl.when(t < tiles - 1)
        def _():
            done = final[pl.ds(pl.multiple_of(lead + t * tile, GROUP), tile), :cols]
            size = jnp.sqrt(jnp.abs(done) * (CODE * CODE / peak[:1, :1]))
            size = jnp.minimum(size + 0.5, CODE).astype(jnp.int32)
            send[t] = jnp.where(done < 0, -size, size).astype(jnp.int16)
            tile_copy(t).start()

    def turn(i, steps):
        fresh, saves = None, []
        for k in range(1, steps + 1):
            fresh, save = advance(k, lead + i * block - GROUP * k, fresh)
            saves.append(save)
        for kept, before, last in filter(None, saves):
            kept[:GROUP, :] = before
            kept[GROUP:, :] = last

    turn(0, min(STEPS, groups))

    @pl.loop(1, tiles // BLOCK + warm)
    def _(i):
        turn(i, STEPS)

        @pl.when(i >= warm)
        def _():
            for n in range(BLOCK):
                finish((i - warm) * BLOCK + n)

    loads[4].wait()
    scale = 1.0 / math.sqrt(MEMBERS - 1)
    for level in range(levels):
        out_i[level] = jnp.zeros((tile, cols), jnp.float32)
    mine = final[lead + (tiles - 1) * tile : lead + tiles * tile, :cols]
    out_i[lax.rem(me, levels)] = pert_in[me].astype(jnp.float32) * (mine * scale)

    @pl.loop(0, tiles - 1)
    def _(t):
        tile_copy(t).wait_recv()
        slab = lax.rem(me - 1 - t + 2 * tiles, tiles)
        peak_copy(t).wait_recv()
        code = recv[t].astype(jnp.float32)
        got = code * jnp.abs(code) * (peaks[t, :1, :1] * (scale / (CODE * CODE)))
        level = lax.rem(slab, levels)
        out_i[level] = out_i[level] + pert_in[slab].astype(jnp.float32) * got

    for edge in edges:
        edge.wait_send()

    @pl.loop(0, tiles)
    def _(t):
        out_copy(t).wait()

    @pl.loop(0, tiles - 1)
    def _(t):
        tile_copy(t).wait_send()
        peak_copy(t).wait_send()


def solution(mesh):
    mems, tys, txs = mesh.shape["mem"], mesh.shape["ty"], mesh.shape["tx"]
    tiles = mems * tys

    def on_device(controls, perturbations, kx, ky, wet):
        rows, cols = kx.shape
        tile = rows // tiles
        levels = tiles // MEMBERS
        wide = cols + LANES
        lead = GROUP * (STEPS + 1)
        deep = lead + rows + GROUP * STEPS
        sides = 1 if txs == 2 else 2
        f32, bf16 = jnp.float32, jnp.bfloat16
        DMA = pltpu.SemaphoreType.DMA
        return pl.pallas_call(
            functools.partial(kernel, mems, tys, txs),
            out_shape=(
                jax.ShapeDtypeStruct((1, rows, cols), f32),
                jax.ShapeDtypeStruct((levels, tile, cols), f32),
            ),
            in_specs=[pl.BlockSpec(memory_space=pltpu.HBM)] * 5,
            out_specs=(pl.BlockSpec(memory_space=pl.ANY), pl.BlockSpec(memory_space=pltpu.VMEM)),
            scratch_shapes=[
                pltpu.VMEM((rows, cols), f32),
                pltpu.VMEM((rows, cols), bf16),
                pltpu.VMEM((rows, cols), bf16),
                pltpu.VMEM((rows, cols), jnp.int32),
                pltpu.VMEM((tiles, tile, cols), bf16),
                pltpu.VMEM((rows, LANES), f32),
                pltpu.VMEM((2, rows, LANES), bf16),
                pltpu.VMEM((sides, rows, LANES), f32),
                pltpu.VMEM((sides, 2, rows, LANES), bf16),
                pltpu.VMEM((rows, wide), f32),
                pltpu.VMEM((rows + GROUP, wide), f32),
                pltpu.VMEM((deep, wide), f32),
                pltpu.VMEM((deep, wide), f32),
                pltpu.VMEM((tiles, tile, cols), jnp.int16),
                pltpu.VMEM((tiles, tile, cols), jnp.int16),
                pltpu.VMEM((GROUP, LANES), f32),
                pltpu.VMEM((tiles, GROUP, LANES), f32),
                DMA((5,)),
                DMA((tiles,)),
                DMA((sides, 2)),
                DMA((sides, 2)),
                DMA((tiles,)),
                DMA((tiles,)),
                DMA((tiles,)),
                DMA((tiles,)),
                pltpu.VMEM((deep, wide), f32),
                pltpu.VMEM((deep, wide), f32),
                *[pltpu.VMEM((2 * GROUP, wide), f32)] * (STEPS - 1),
            ],
            compiler_params=pltpu.CompilerParams(
                collective_id=0, has_side_effects=True, vmem_limit_bytes=63 * 2**20
            ),
        )(controls, perturbations, kx, ky, wet)

    in_specs = (
        P(("mem", "ty"), None, "tx"),
        P(None, ("mem", "ty"), "tx"),
        P(None, "tx"),
        P(None, "tx"),
        P(None, "tx"),
    )
    out_specs = (P(("mem", "ty"), None, "tx"), P(None, ("mem", "ty"), "tx"))
    return jax.shard_map(
        on_device, mesh=mesh, in_specs=in_specs, out_specs=out_specs, check_vma=False
    )
```
